128 devices in a mesh: row: 4 (over x_hi, core), col: 32 (over y, x_lo, z).
Axes of the slice: x: 4 (x_hi: 2, x_lo: 2; x = x_hi * 2 + x_lo), y: 4, z: 4, core: 2. Of those that a mesh axis runs over, the one named last changes fastest.
Arguments:
- tokens: bfloat16 [49152, 2048], P('col', 'row'), may hold values from -6 to 6
- in_weight: float32 [2048, 6144], P(('row', 'col')), may hold values from -0.125 to 0.125
- out_weight: float32 [2048, 2048], P(('row', 'col')), may hold values from -0.125 to 0.125
- beta_weight: float32 [2048, 16], replicated, may hold values from -0.25 to 0.25
- conv_weight: float32 [4, 6144], P(None, 'row'), may hold values from -2.5 to 2.5
- conv_prior: bfloat16 [96, 3, 6144], P('col', None, 'row'), may hold values from -6 to 6
- head_gain: float32 [2048], P('row'), may hold values from 0.1 to 1.9
- state_pool: float32 [192, 16, 128, 128], P('col', 'row'), may hold values from -2.5 to 2.5
- state_index: int32 [96, 16], P('col', 'row'), may hold values from 0 to 5
- lengths: int32 [96], P('col'), may hold values from 1 to 512, 36864 in all
- page_table: int32 [96, 4, 2], P('col'), may hold values from 0 to 31, as said below
Outputs:
- server_in: bfloat16 [2048, 6144], P('row', 'col')
- server_out: bfloat16 [2048, 2048], P('row', 'col')
- layer_out: bfloat16 [49152, 2048], P('col', 'row')
- final_state: float32 [96, 16, 128, 128], P('col', 'row')
- page_cache: bfloat16 [384, 128, 2, 2048], P('col', None, None, 'row')
The draws below stay inside these ranges and needn't reach their ends.
Inputs may be any that keep to these rules, and one draw needn't show every extreme that they name: `lengths`: one prompt has all 512 tokens live. `state_index`: which of its own index of col's 6 stored states a prompt and head continues. page_table[p, g, 0] is the index of col that keeps page g of prompt p and page_table[p, g, 1] its slot there, below 12; every slot of every index of col gets exactly one page; the prompts of one index of col send at most 1 pages to any one index of col, and exactly 1 to some.
All inputs are finite; a program needn't handle non-finite values. No bound on the sum of `lengths` on one device may be relied on, other than what follows from the above.
Results may differ from the reference program's by a relative error of at most 0.029.
Values may be sent and summed in bfloat16 or wider, within the bound.
No kernel may reach another device: no remote copies, remote signals or barrier semaphores. Data moves between devices by JAX's collectives and lax.ppermute only.
A program may use at most 128 MiB of HBM per device.

```python
import math
import jax
import jax.numpy as jnp
import numpy as np
from jax import lax

D = 2048
HEADS = 16
DK = 128
STRETCH = 64
CONV = 4
SEQ = 512
PAGE = 128
PR_DEV = 3
PROMPTS = 96
TOKENS = 49152
QKV = 6144
HD = 2048
PAGES_SEQ = 4
PAGES_DEV = 12
CAP = 1
POOL_DEV = 6
N_ROW = 4
N_COL = 32


def draw_page_table(key, part):
    offset = jax.random.randint(jax.random.fold_in(key, 7), (), 0, N_COL)
    subkeys = jax.random.split(jax.random.fold_in(key, 11), N_COL)
    ranking = jax.vmap(lambda subkey: jax.random.permutation(subkey, PAGES_DEV))(subkeys).astype(jnp.int32)
    source = jnp.arange(N_COL, dtype=jnp.int32)[:, None]
    target = (source + ranking // CAP + offset) % N_COL
    entries = jnp.stack([target, ranking], axis=-1).astype(jnp.int32)
    return entries.reshape(PROMPTS, PAGES_SEQ, 2)


def touch_ends(values, key, smallest, largest):
    shape = values.shape
    spot = [jax.random.randint(jax.random.fold_in(key, axis), (), 0, shape[axis]) for axis in range(len(shape))]
    values = values.at[tuple(spot)].set(smallest)
    longest = shape.index(max(shape))
    spot[longest] = (spot[longest] + 1) % shape[longest]
    return values.at[tuple(spot)].set(largest)


def block_scale(own_key, shape, shards, low, largest):
    level = 1.0
    for position, blocks in shards:
        steps = jax.random.uniform(jax.random.fold_in(jax.random.fold_in(own_key, 6), position), (blocks,), jnp.float32, low / len(shards), largest / len(shards))
        level = level * jnp.repeat(jnp.exp(steps), shape[position] // blocks).reshape((-1,) + (1,) * (len(shape) - 1 - position))
    return level


def length_profile(amount, total, reach, slope):
    portions = [(1 << 20) // math.isqrt(rank ** slope) + 1 for rank in range(2, amount + 1)]
    spare, given = total - reach - (amount - 1), [1] * (amount - 1)
    while spare > 0:
        movable = [i for i in range(amount - 1) if given[i] < reach]
        whole, budget = sum([portions[i] for i in movable]), spare
        for i in movable:
            more = min(reach - given[i], max(1, budget * portions[i] // whole), spare)
            given[i] = given[i] + more
            spare = spare - more
    return np.array([reach] + given)


def ragged(key, count, total, reach, skew):
    if count == 2:
        one = jax.random.randint(key, (), max(1, total - reach), min(reach, total - 1) + 1)
        return jnp.stack([one, total - one])
    sizes = jnp.asarray(length_profile(count, total, reach, skew), jnp.int32)
    pairs = (count - 1) // 2
    donor, taker = sizes[1:1 + 2 * pairs:2], sizes[2:2 + 2 * pairs:2]
    margin = jnp.minimum(donor - 1, reach - taker)
    shifted = jax.random.randint(jax.random.fold_in(key, 1), (pairs,), 0, 1 << 20) % (margin + 1)
    sizes = sizes.at[1:1 + 2 * pairs:2].set(donor - shifted).at[2:2 + 2 * pairs:2].set(taker + shifted)
    return sizes[jax.random.permutation(jax.random.fold_in(key, 2), count)]


def scatter_about(rng, dims, width, bound, pieces=(), kind=jnp.bfloat16):
    loudness = block_scale(rng, dims, pieces, -0.22, 0.18) if pieces else 1.0
    array = jax.random.normal(rng, dims, jnp.float32) * width * loudness
    return jnp.minimum(jnp.maximum(array, -bound), bound).astype(kind)


def setup_inputs(seed: int = 0) -> dict:
    splits = jax.random.split(jax.random.key(seed), 12)
    tokens = scatter_about(splits[0], (TOKENS, D), 1.0, 6.0, ((0, 32), (1, 4)))
    in_weight = scatter_about(splits[1], (D, QKV), D ** -0.5, 0.125, ((0, 128),), jnp.float32)
    out_weight = scatter_about(splits[2], (HD, D), HD ** -0.5, 0.125, ((0, 128),), jnp.float32)
    beta_weight = scatter_about(splits[3], (D, HEADS), (D // 4) ** -0.5, 0.25, (), jnp.float32)
    conv_weight = scatter_about(splits[4], (CONV, QKV), 0.5, 2.5, ((1, 4),), jnp.float32)
    conv_prior = scatter_about(splits[5], (PROMPTS, CONV - 1, QKV), 1.0, 6.0, ((0, 32), (2, 4)))
    head_gain = jnp.clip(1.0 + 0.18 * jax.random.normal(splits[6], (HD,), jnp.float32), 0.1, 1.9)
    state_pool = scatter_about(splits[7], (N_COL * POOL_DEV, HEADS, DK, DK), 0.25, 2.5, ((0, 32), (1, 4)), jnp.float32)
    state_index = touch_ends(jax.random.randint(splits[8], (PROMPTS, HEADS), 0, POOL_DEV), jax.random.fold_in(splits[8], 1), 0, POOL_DEV - 1).astype(jnp.int32)
    lengths = ragged(splits[9], PROMPTS, PROMPTS * SEQ * 3 // 4, SEQ, 2).astype(jnp.int32)
    page_table = draw_page_table(jax.random.fold_in(splits[11], 71), 0)
    return {"tokens": tokens, "in_weight": in_weight, "out_weight": out_weight, "beta_weight": beta_weight, "conv_weight": conv_weight, "conv_prior": conv_prior, "head_gain": head_gain, "state_pool": state_pool, "state_index": state_index, "lengths": lengths, "page_table": page_table}


HIGHEST = lax.Precision.HIGHEST

def delta_block(carry_state, block_data):
    query_unit, key_unit, values, beta_rates = block_data
    width_c = beta_rates.shape[1]
    width_k = key_unit.shape[2]
    strict_lower = jnp.tril(jnp.ones((width_c, width_c), jnp.float32), -1)
    causal = jnp.tril(jnp.ones((width_c, width_c), jnp.float32))
    gram_matrix = jnp.einsum('bik,bjk->bij', key_unit, key_unit, precision=HIGHEST)
    system = jnp.eye(width_c, dtype=jnp.float32) + beta_rates[:, :, None] * gram_matrix * strict_lower
    right_side = jnp.concatenate([key_unit, values], axis=2) * beta_rates[:, :, None]
    solved = jax.scipy.linalg.solve_triangular(system, right_side, lower=True, unit_diagonal=True)
    weighted = solved[:, :, :width_k]
    corrected = solved[:, :, width_k:] - jnp.einsum('bck,bkv->bcv', weighted, carry_state, precision=HIGHEST)
    scores = jnp.einsum('bik,bjk->bij', query_unit, key_unit, precision=HIGHEST) * causal
    output = jnp.einsum('bck,bkv->bcv', query_unit, carry_state, precision=HIGHEST) + jnp.einsum('bij,bjv->biv', scores, corrected, precision=HIGHEST)
    carry_state = carry_state + jnp.einsum('bck,bcv->bkv', key_unit, corrected, precision=HIGHEST)
    return (carry_state, output)

def delta_scan(query_unit, key_unit, values, beta_rates, initial, block_len):
    batch_n = query_unit.shape[0]
    length_all = query_unit.shape[1]
    num_blocks = length_all // block_len

    def to_blocks(tensor):
        shaped = tensor.reshape((batch_n, num_blocks, block_len) + tensor.shape[2:])
        return jnp.moveaxis(shaped, 1, 0)
    last_state, outputs = lax.scan(delta_block, initial, (to_blocks(query_unit), to_blocks(key_unit), to_blocks(values), to_blocks(beta_rates)))
    outputs = jnp.moveaxis(outputs, 0, 1).reshape(batch_n, length_all, -1)
    return (last_state, outputs)

def unit_rows(tensor):
    return tensor * lax.rsqrt(lax.optimization_barrier(jnp.sum(tensor * tensor, axis=-1, keepdims=True)) + 1e-06)

def blockwise_product(left, right, groups):
    span_rows = left.shape[1] // groups
    running = jnp.zeros((left.shape[0], right.shape[1]), jnp.float32)
    for group_id in range(groups):
        piece_sum = jnp.dot(left[:, group_id * span_rows:(group_id + 1) * span_rows].astype(jnp.float32), right[group_id * span_rows:(group_id + 1) * span_rows].astype(jnp.float32), preferred_element_type=jnp.float32).astype(jnp.bfloat16)
        running = running + lax.optimization_barrier(piece_sum).astype(jnp.float32)
    return running.astype(jnp.bfloat16)

def reference(tokens, in_weight, out_weight, beta_weight, conv_weight, conv_prior, head_gain, state_pool, state_index, lengths, page_table):
    server_in = in_weight.astype(jnp.bfloat16)
    server_out = out_weight.astype(jnp.bfloat16)
    beta_cast = beta_weight.astype(jnp.bfloat16)
    prompt_ids = jnp.arange(PROMPTS, dtype=jnp.int32)
    pool_rows = (prompt_ids // PR_DEV * POOL_DEV)[:, None] + state_index
    initial = state_pool[pool_rows, jnp.arange(HEADS, dtype=jnp.int32)[None, :]]

    def prompt_layer(inputs):
        prompt_tokens, prior_rows, live_len, start_state = inputs
        live_mask = (jnp.arange(SEQ, dtype=jnp.int32) < live_len).astype(jnp.float32)
        projected = blockwise_product(prompt_tokens, server_in, N_ROW)
        beta_rates = live_mask[:, None] * jax.nn.sigmoid(jnp.dot(prompt_tokens.astype(jnp.float32), beta_cast.astype(jnp.float32), preferred_element_type=jnp.float32))
        padded = jnp.concatenate([prior_rows.astype(jnp.float32), projected.astype(jnp.float32)], axis=0)
        conv_sum = jnp.zeros((SEQ, QKV), jnp.float32)
        for tap_id in range(CONV):
            conv_sum = conv_sum + conv_weight[tap_id][None, :] * padded[tap_id:tap_id + SEQ]
        activated = jax.nn.silu(conv_sum).reshape(SEQ, HEADS, 3, DK).transpose(1, 2, 0, 3)
        query_unit = unit_rows(activated[:, 0])
        key_unit = unit_rows(activated[:, 1])
        values = activated[:, 2]
        last_state, outputs = delta_scan(query_unit, key_unit, values, beta_rates.T, start_state, STRETCH)
        outputs = outputs * live_mask[None, :, None]
        normed = outputs * lax.rsqrt(lax.optimization_barrier(jnp.mean(outputs * outputs, axis=2, keepdims=True)) + 1e-05) * head_gain.reshape(HEADS, 1, DK)
        normed = normed.astype(jnp.bfloat16).transpose(1, 0, 2).reshape(SEQ, HD)
        mixed_rows = blockwise_product(normed, server_out, N_ROW)
        keep_mask = live_mask[None, :, None]
        kept_pairs = jnp.stack([key_unit * keep_mask, values * keep_mask], axis=0)
        page_rows = kept_pairs.transpose(2, 0, 1, 3).reshape(PAGES_SEQ, PAGE, 2, HD).astype(jnp.bfloat16)
        return (mixed_rows, last_state, page_rows)
    mixed_all, state_all, page_all = lax.map(prompt_layer, (tokens.reshape(PROMPTS, SEQ, D), conv_prior, lengths, initial))
    targets = (page_table[:, :, 0] * PAGES_DEV + page_table[:, :, 1]).reshape(-1)
    page_cache = jnp.zeros((N_COL * PAGES_DEV, PAGE, 2, HD), jnp.bfloat16).at[targets].set(page_all.reshape(PROMPTS * PAGES_SEQ, PAGE, 2, HD))
    return (server_in, server_out, mixed_all.reshape(TOKENS, D), state_all, page_cache)
```

```python
import functools
import jax
import jax.numpy as jnp
from jax import lax
from jax.experimental import pallas as pl
from jax.experimental.pallas import tpu as pltpu
from jax.sharding import PartitionSpec as P

DK = 128
CONV = 4
SEQ = 512
PAGE = 128
PAGES_SEQ = 4
CHUNK = 128
ROWS = 4
XORS = (0, 2, 1, 3)
BF = jnp.bfloat16
F32 = jnp.float32


def mm(a, b, dims=((1,), (0,))):
    return lax.dot_general(a, b, (dims, ((), ())), preferred_element_type=F32)


def assemble(w_ref, scratch, cols):
    n_col = w_ref.shape[0]
    for c in range(n_col):
        for r in range(ROWS):
            scratch[r, c * 16 : (c + 1) * 16, :] = w_ref[c, r * 16 : (r + 1) * 16, :]


def proj_kernel(
    targets,
    lens,
    tok_ref,
    w_ref,
    beta_ref,
    taps_ref,
    prior_ref,
    q_ref,
    k_ref,
    v_ref,
    rate_ref,
    page_ref,
    w_scr,
    u_scr,
    kv_scr,
):
    prompt, pair, page = pl.program_id(1), pl.program_id(0), pl.program_id(2)
    width = u_scr.shape[1]

    @pl.when((prompt == 0) & (page == 0))
    def _():
        assemble(w_ref, w_scr, width)

    @pl.when(page == 0)
    def _():
        acc = mm(tok_ref[0], w_scr[0])
        for r in range(1, ROWS):
            acc += mm(tok_ref[r], w_scr[r])
        u_scr[8:, :] = acc
        u_scr[0:8, :] = prior_ref[0]

    @pl.when((page == 0) & (pair == 0))
    def _():
        logits = mm(tok_ref[0], beta_ref[0])
        for r in range(1, ROWS):
            logits += mm(tok_ref[r], beta_ref[r])
        rows = lax.broadcasted_iota(jnp.int32, (SEQ, DK), 0)
        live = rows < lens[prompt]
        rate_ref[...] = jnp.where(live, jax.nn.sigmoid(logits), 0.0)

    base = page * PAGE
    rows = base + lax.broadcasted_iota(jnp.int32, (PAGE, DK), 0)
    live = rows < lens[prompt]
    window = u_scr[pl.ds(pl.multiple_of(base, PAGE), PAGE + 8), :]
    heads = width // (3 * DK)
    for h in range(heads):
        for j in range(3):
            lo = (3 * h + j) * DK
            win = window[:, lo : lo + DK]
            total = taps_ref[0, lo : lo + DK][None, :] * win[5 : 5 + PAGE]
            for i in range(1, CONV):
                total += taps_ref[i, lo : lo + DK][None, :] * win[5 + i : 5 + i + PAGE]
            act = total * jax.nn.sigmoid(total)
            if j < 2:
                act = act * lax.rsqrt(jnp.sum(act * act, axis=1, keepdims=True) + 1e-06)
            if j == 0:
                q_ref[h] = act.astype(BF)
            else:
                act = jnp.where(live, act, 0.0)
                (k_ref, v_ref)[j - 1][h] = act.astype(BF)
                kv_scr[h, pl.ds(j - 1, PAGE, stride=2), :] = act
    for h in range(heads):
        page_ref[0, :, h * DK : (h + 1) * DK] = kv_scr[h].astype(BF)


def project(targets, lens, tok, w, beta, taps, prior, n_slots):
    prompts = lens.shape[0]
    n_cols = w.shape[2]
    heads = n_cols // (3 * DK)
    pair_n = 2
    pairs = heads // pair_n
    width = pair_n * 3 * DK
    grid_spec = pltpu.PrefetchScalarGridSpec(
        num_scalar_prefetch=2,
        grid=(pairs, prompts, PAGES_SEQ),
        in_specs=[
            pl.BlockSpec((ROWS, SEQ, tok.shape[2]), lambda a, p, g, t, n: (0, p, 0)),
            pl.BlockSpec((w.shape[0], w.shape[1], width), lambda a, p, g, t, n: (0, 0, a)),
            pl.BlockSpec(beta.shape, lambda a, p, g, t, n: (0, 0, 0)),
            pl.BlockSpec((CONV, width), lambda a, p, g, t, n: (0, a)),
            pl.BlockSpec((1, 8, width), lambda a, p, g, t, n: (p, 0, a)),
        ],
        out_specs=[
            pl.BlockSpec((pair_n, PAGE, DK), lambda a, p, g, t, n: (a, p * PAGES_SEQ + g, 0)),
            pl.BlockSpec((pair_n, PAGE, DK), lambda a, p, g, t, n: (a, p * PAGES_SEQ + g, 0)),
            pl.BlockSpec((pair_n, PAGE, DK), lambda a, p, g, t, n: (a, p * PAGES_SEQ + g, 0)),
            pl.BlockSpec((SEQ, DK), lambda a, p, g, t, n: (jnp.where(a == 0, p, prompts), 0)),
            pl.BlockSpec(
                (1, 2 * PAGE, pair_n * DK), lambda a, p, g, t, n: (t[p * PAGES_SEQ + g], 0, a)
            ),
        ],
        scratch_shapes=[
            pltpu.VMEM((ROWS, w.shape[0] * 16, width), BF),
            pltpu.VMEM((SEQ + 8, width), F32),
            pltpu.VMEM((pair_n, 2 * PAGE, DK), F32),
        ],
    )
    total = prompts * SEQ
    return pl.pallas_call(
        proj_kernel,
        grid_spec=grid_spec,
        out_shape=[
            jax.ShapeDtypeStruct((heads, total, DK), BF),
            jax.ShapeDtypeStruct((heads, total, DK), BF),
            jax.ShapeDtypeStruct((heads, total, DK), BF),
            jax.ShapeDtypeStruct((total + SEQ, DK), F32),
            jax.ShapeDtypeStruct((n_slots, 2 * PAGE, heads * DK), BF),
        ],
        compiler_params=pltpu.CompilerParams(vmem_limit_bytes=48 << 20),
        cost_estimate=pl.CostEstimate(
            flops=2 * total * 2048 * n_cols, bytes_accessed=24 << 20, transcendentals=total * n_cols
        ),
        name="project",
    )(targets, lens, tok, w, beta, taps, prior)


def scan_kernel(lens, index, q_ref, k_ref, v_ref, rate_ref, gain_ref, *rest):
    heads = q_ref.shape[0]
    starts, (out_ref, state_ref) = rest[:heads], rest[heads:]
    prompt = pl.program_id(0)
    n_chunk = SEQ // CHUNK
    ri = lax.broadcasted_iota(jnp.int32, (CHUNK, CHUNK), 0)
    ci = lax.broadcasted_iota(jnp.int32, (CHUNK, CHUNK), 1)
    diff = ri ^ ci
    lower = ri > ci
    eye = (ri == ci).astype(F32)
    causal = ri >= ci
    states = [starts[h][0, 0] for h in range(heads)]
    for c in range(n_chunk):
        rows = slice(c * CHUNK, (c + 1) * CHUNK)
        live = (c * CHUNK + ri) < lens[prompt]
        q = [q_ref[h, rows, :] for h in range(heads)]
        k = [k_ref[h, rows, :] for h in range(heads)]
        rate = [rate_ref[rows, h : h + 1] for h in range(heads)]
        gram = [mm(k[h], k[h], ((1,), (1,))) for h in range(heads)]
        strict = [jnp.where(lower, gram[h] * rate[h], 0.0) for h in range(heads)]
        inv = [eye - jnp.where(diff == 1, strict[h], 0.0) for h in range(heads)]
        level = 1
        while (2 << level) <= CHUNK:
            part = [
                jnp.where((diff >> level) == 1, strict[h], 0.0).astype(BF) for h in range(heads)
            ]
            low = [inv[h].astype(BF) for h in range(heads)]
            mid = [mm(part[h], low[h]).astype(BF) for h in range(heads)]
            inv = [inv[h] - mm(low[h], mid[h]) for h in range(heads)]
            level += 1
        scores = [
            jnp.where(causal, mm(q[h], k[h], ((1,), (1,))), 0.0).astype(BF) for h in range(heads)
        ]
        kf = [k[h].astype(F32) * rate[h] for h in range(heads)]
        vf = [v_ref[h, rows, :].astype(F32) * rate[h] for h in range(heads)]
        right = [jnp.concatenate([kf[h].astype(BF), vf[h].astype(BF)], axis=1) for h in range(heads)]
        solved = [mm(inv[h].astype(BF), right[h]) for h in range(heads)]
        for h in range(heads):
            sb = states[h].astype(BF)
            wq = jnp.concatenate([solved[h][:, :DK].astype(BF), q[h]], axis=0)
            both = mm(wq, sb)
            fixed = (solved[h][:, DK:] - both[:CHUNK]).astype(BF)
            out = both[CHUNK:] + mm(scores[h], fixed)
            states[h] = states[h] + mm(k[h], fixed, ((0,), (0,)))
            out = jnp.where(live, out, 0.0)
            scale = lax.rsqrt(jnp.mean(out * out, axis=1, keepdims=True) + 1e-05)
            gain = gain_ref[0:1, h * DK : (h + 1) * DK]
            out_ref[rows, h * DK : (h + 1) * DK] = (out * scale * gain).astype(BF)
    for h in range(heads):
        state_ref[0, h] = states[h]


def scan_all(lens, index, q, k, v, rate, gain, pool):
    heads = q.shape[0]
    prompts = lens.shape[0]
    qkv = pl.BlockSpec((heads, SEQ, DK), lambda p, n, i: (0, p, 0))

    def start_spec(h):
        return pl.BlockSpec((1, 1, DK, DK), lambda p, n, i: (i[p * heads + h], h, 0, 0))

    grid_spec = pltpu.PrefetchScalarGridSpec(
        num_scalar_prefetch=2,
        grid=(prompts,),
        in_specs=[
            qkv,
            qkv,
            qkv,
            pl.BlockSpec((SEQ, DK), lambda p, n, i: (p, 0)),
            pl.BlockSpec((1, heads * DK), lambda p, n, i: (0, 0)),
        ]
        + [start_spec(h) for h in range(heads)],
        out_specs=[
            pl.BlockSpec((SEQ, heads * DK), lambda p, n, i: (p, 0)),
            pl.BlockSpec((1, heads, DK, DK), lambda p, n, i: (p, 0, 0, 0)),
        ],
    )
    return pl.pallas_call(
        scan_kernel,
        grid_spec=grid_spec,
        out_shape=[
            jax.ShapeDtypeStruct((prompts * SEQ, heads * DK), BF),
            jax.ShapeDtypeStruct((prompts, heads, DK, DK), F32),
        ],
        compiler_params=pltpu.CompilerParams(vmem_limit_bytes=40 << 20),
        cost_estimate=pl.CostEstimate(
            flops=24 << 30, bytes_accessed=12 << 20, transcendentals=0
        ),
        name="delta",
    )(lens, index, q, k, v, rate, gain, *([pool] * heads))


def out_kernel(x_ref, w_ref, o_ref, w_scr):
    @pl.when(pl.program_id(0) == 0)
    def _():
        assemble(w_ref, w_scr, w_scr.shape[2])

    acc = mm(x_ref[0], w_scr[0])
    for r in range(1, ROWS):
        acc += mm(x_ref[r], w_scr[r])
    o_ref[...] = acc.astype(BF)


def out_product(x, w):
    total, n_cols = x.shape[1], w.shape[2]
    return pl.pallas_call(
        out_kernel,
        grid=(total // SEQ,),
        in_specs=[
            pl.BlockSpec((ROWS, SEQ, x.shape[2]), lambda p: (0, p, 0)),
            pl.BlockSpec(w.shape, lambda p: (0, 0, 0)),
        ],
        out_specs=pl.BlockSpec((SEQ, n_cols), lambda p: (p, 0)),
        out_shape=jax.ShapeDtypeStruct((total, n_cols), BF),
        scratch_shapes=[pltpu.VMEM((ROWS, w.shape[0] * 16, n_cols), BF)],
        compiler_params=pltpu.CompilerParams(vmem_limit_bytes=32 << 20),
        cost_estimate=pl.CostEstimate(
            flops=2 * total * 2048 * n_cols, bytes_accessed=10 << 20, transcendentals=0
        ),
        name="outmix",
    )(x, w)


def row_swap(x, k):
    return lax.ppermute(x, "row", [(r, r ^ k) for r in range(ROWS)])


def row_gather(x):
    near = row_swap(x, 2)
    mine = jnp.stack([x, near])
    return jnp.concatenate([mine, row_swap(mine, 1)], axis=0)


def col_gather(x):
    n_col = lax.axis_size("col")
    return lax.all_to_all(
        jnp.broadcast_to(x[None], (n_col,) + x.shape), "col", split_axis=0, concat_axis=0, tiled=True
    )


def local(
    tokens,
    in_weight,
    out_weight,
    beta_weight,
    conv_weight,
    conv_prior,
    head_gain,
    state_pool,
    state_index,
    lengths,
    page_table,
):
    n_col = lax.axis_size("col")
    row_id = lax.axis_index("row")
    span = tokens.shape[1]
    heads = state_index.shape[1]
    prompts = lengths.shape[0]
    n_pages = prompts * PAGES_SEQ
    part = in_weight.shape[0]
    in_cols = in_weight.shape[1] // ROWS
    out_cols = out_weight.shape[1] // ROWS

    win = in_weight.astype(BF)
    wout = out_weight.astype(BF)
    both = jnp.concatenate(
        [win.reshape(part, ROWS, in_cols), wout.reshape(part, ROWS, out_cols)], axis=2
    ).transpose(1, 0, 2)

    def piece(r):
        return lax.dynamic_index_in_dim(both, r, 0, keepdims=False)

    pieces = [piece(row_id)] + [row_swap(piece(row_id ^ k), k) for k in XORS[1:]]
    mine = jnp.concatenate(pieces, axis=0)
    wide_in = col_gather(mine[:, :in_cols])
    wide_out = col_gather(mine[:, in_cols:])

    tok_all = row_gather(tokens)

    targets = page_table[:, :, 0].reshape(-1)
    slots = page_table[:, :, 1].reshape(-1)
    hit = targets[:, None] == jnp.arange(n_col, dtype=jnp.int32)[None, :]
    slot_for = jnp.max(jnp.where(hit, slots[:, None], -1), axis=0)
    block_in, block_out = win.shape[1] // n_col, wout.shape[1] // n_col
    send = jnp.concatenate(
        [
            win.reshape(part, n_col, block_in).transpose(1, 0, 2).reshape(n_col, -1, DK),
            wout.reshape(part, n_col, block_out).transpose(1, 0, 2).reshape(n_col, -1, DK),
            jnp.broadcast_to(slot_for.astype(BF)[:, None, None], (n_col, 8, DK)),
        ],
        axis=1,
    )
    got = lax.all_to_all(send, "col", split_axis=0, concat_axis=0, tiled=True)
    n_in = part * block_in // DK
    n_out = part * block_out // DK
    server_in = got[:, :n_in].reshape(n_col * part, block_in)
    server_out = got[:, n_in : n_in + n_out].reshape(n_col * part, block_out)
    arrived_slots = got[:, n_in + n_out, 0].astype(jnp.int32)
    wanted = arrived_slots[None, :] == jnp.arange(n_pages, dtype=jnp.int32)[:, None]
    source = jnp.sum(
        jnp.where(wanted, jnp.arange(n_col, dtype=jnp.int32)[None, :], 0), axis=1
    ).astype(jnp.int32)

    beta = lax.dynamic_slice_in_dim(beta_weight, row_id * heads, heads, 1).astype(BF)
    beta = beta.reshape(ROWS, span, heads)
    beta = jnp.stack(
        [lax.dynamic_index_in_dim(beta, row_id ^ k, 0, keepdims=False) for k in XORS]
    )
    beta = jnp.pad(beta, ((0, 0), (0, 0), (0, DK - heads)))
    prior = jnp.pad(conv_prior.astype(F32), ((0, 0), (8 - (CONV - 1), 0), (0, 0)))

    q, k, v, rate, outgoing = project(
        targets, lengths, tok_all, wide_in, beta, conv_weight, prior, n_col
    )
    arrived = lax.all_to_all(outgoing, "col", split_axis=0, concat_axis=0, tiled=True)
    normed, final_state = scan_all(
        lengths, state_index.reshape(-1), q, k, v, rate, head_gain.reshape(1, -1), state_pool
    )
    layer_out = out_product(row_gather(normed), wide_out)
    page_cache = jnp.take(arrived, source, axis=0, mode="clip").reshape(
        n_pages, PAGE, 2, heads * DK
    )
    return (server_in, server_out, layer_out, final_state, page_cache)


def solution(mesh):
    return jax.shard_map(
        local,
        mesh=mesh,
        in_specs=(
            P("col", "row"),
            P(("row", "col"), None),
            P(("row", "col"), None),
            P(),
            P(None, "row"),
            P("col", None, "row"),
            P("row"),
            P("col", "row", None, None),
            P("col", "row"),
            P("col"),
            P("col", None, None),
        ),
        out_specs=(
            P("row", "col"),
            P("row", "col"),
            P("col", "row"),
            P("col", "row", None, None),
            P("col", None, None, "row"),
        ),
        check_vma=False,
    )
```

```python
import functools
import jax
import jax.numpy as jnp
from jax import lax
from jax.experimental import pallas as pl
from jax.experimental.pallas import tpu as pltpu
from jax.sharding import PartitionSpec as P

DK = 128
CONV = 4
SEQ = 512
PAGE = 128
PAGES_SEQ = 4
CHUNK = 128
ROWS = 4
XORS = (0, 2, 1, 3)
BF = jnp.bfloat16
F32 = jnp.float32


def mm(a, b, dims=((1,), (0,))):
    return lax.dot_general(a, b, (dims, ((), ())), preferred_element_type=F32)


def assemble(spots, pieces, scratch, col=None):
    j = 0
    width = pieces[0].shape[2]
    for ref in pieces:
        for i in range(ref.shape[0]):
            at = pl.ds(pl.multiple_of(spots[j] * 16, 16), 16)
            for r in range(ROWS):
                block = ref[i, r * 16 : (r + 1) * 16, :]
                if col is None:
                    scratch[r, at, :] = block
                else:
                    scratch[r, at, col : col + width] = block
            j += 1


def proj_kernel(with_rate, n_piece, n_after, targets, lens, spots, *refs):
    toks, refs = refs[:ROWS], refs[ROWS:]
    pieces, refs = refs[:n_piece], refs[n_piece:]
    if with_rate:
        beta_ref, refs = refs[0], refs[1:]
    refs = refs[:2] + refs[2 + n_after :]
    taps_ref, prior_ref, q_ref, k_ref, v_ref, page_ref = refs[:6]
    if with_rate:
        rate_ref = refs[6]
    w_scr, u_scr, kv_scr = refs[-3:]
    prompt, page = pl.program_id(0), pl.program_id(1)
    width = u_scr.shape[1]

    @pl.when((prompt == 0) & (page == 0))
    def _():
        assemble(spots, pieces, w_scr)

    @pl.when(page == 0)
    def _():
        acc = mm(toks[0][...], w_scr[0])
        for r in range(1, ROWS):
            acc += mm(toks[r][...], w_scr[r])
        u_scr[8:, :] = acc
        u_scr[0:8, :] = prior_ref[0]
        if with_rate:
            logits = mm(toks[0][...], beta_ref[0])
            for r in range(1, ROWS):
                logits += mm(toks[r][...], beta_ref[r])
            spot = lax.broadcasted_iota(jnp.int32, (SEQ, DK), 0)
            rate_ref[...] = jnp.where(spot < lens[prompt], jax.nn.sigmoid(logits), 0.0)

    base = page * PAGE
    live = base + lax.broadcasted_iota(jnp.int32, (PAGE, DK), 0) < lens[prompt]
    window = u_scr[pl.ds(pl.multiple_of(base, PAGE), PAGE + 8), :]
    heads = width // (3 * DK)
    for h in range(heads):
        for j in range(3):
            lo = (3 * h + j) * DK
            win = window[:, lo : lo + DK]
            total = taps_ref[0, lo : lo + DK][None, :] * win[5 : 5 + PAGE]
            for i in range(1, CONV):
                total += taps_ref[i, lo : lo + DK][None, :] * win[5 + i : 5 + i + PAGE]
            act = total * jax.nn.sigmoid(total)
            if j < 2:
                act = act * lax.rsqrt(jnp.sum(act * act, axis=1, keepdims=True) + 1e-06)
            if j == 0:
                q_ref[h] = act.astype(BF)
            else:
                act = jnp.where(live, act, 0.0)
                (k_ref, v_ref)[j - 1][h] = act.astype(BF)
                kv_scr[h, pl.ds(j - 1, PAGE, stride=2), :] = act
    for h in range(heads):
        page_ref[0, :, h * DK : (h + 1) * DK] = kv_scr[h].astype(BF)


def project(pair, targets, lens, spots, toks, pieces, beta, taps, prior, n_slots, after=()):
    prompts = lens.shape[0]
    pair_n = 2
    width = pair_n * 3 * DK
    with_rate = beta is not None
    total = prompts * SEQ
    span = toks[0].shape[1]

    def whole(x):
        return pl.BlockSpec((x.shape[0], x.shape[1], width), lambda p, g, t, n, c: (0, 0, 0))

    in_specs = [pl.BlockSpec((SEQ, span), lambda p, g, t, n, c: (p, 0))] * ROWS
    in_specs += [whole(x) for x in pieces]
    operands = [*toks, *pieces]
    if with_rate:
        in_specs += [pl.BlockSpec(beta.shape, lambda p, g, t, n, c: (0, 0, 0))]
        operands += [beta]
    in_specs += [
        pl.BlockSpec((CONV, width), lambda p, g, t, n, c: (0, pair)),
        pl.BlockSpec((1, 8, width), lambda p, g, t, n, c: (p, 0, pair)),
    ]
    in_specs += [pl.BlockSpec(memory_space=pl.ANY)] * len(after)
    operands += [taps, prior, *after]
    head_spec = pl.BlockSpec((pair_n, PAGE, DK), lambda p, g, t, n, c: (0, p * PAGES_SEQ + g, 0))
    out_specs = [head_spec] * 3 + [
        pl.BlockSpec((1, 2 * PAGE, pair_n * DK), lambda p, g, t, n, c: (t[p * PAGES_SEQ + g], 0, 0))
    ]
    out_shape = [jax.ShapeDtypeStruct((pair_n, total, DK), BF)] * 3 + [
        jax.ShapeDtypeStruct((n_slots, 2 * PAGE, pair_n * DK), BF)
    ]
    if with_rate:
        out_specs += [pl.BlockSpec((SEQ, DK), lambda p, g, t, n, c: (p, 0))]
        out_shape += [jax.ShapeDtypeStruct((total, DK), F32)]
    grid_spec = pltpu.PrefetchScalarGridSpec(
        num_scalar_prefetch=3,
        grid=(prompts, PAGES_SEQ),
        in_specs=in_specs,
        out_specs=out_specs,
        scratch_shapes=[
            pltpu.VMEM((ROWS, spots.shape[0] * 16, width), BF),
            pltpu.VMEM((SEQ + 8, width), F32),
            pltpu.VMEM((pair_n, 2 * PAGE, DK), F32),
        ],
    )
    return pl.pallas_call(
        functools.partial(proj_kernel, with_rate, len(pieces), len(after)),
        grid_spec=grid_spec,
        out_shape=out_shape,
        compiler_params=pltpu.CompilerParams(vmem_limit_bytes=56 << 20),
        cost_estimate=pl.CostEstimate(
            flops=2 * total * 2048 * width, bytes_accessed=14 << 20, transcendentals=total * width
        ),
        name="project",
    )(targets, lens, spots, *operands)


def scan_kernel(pair, lens, index, q_ref, k_ref, v_ref, rate_ref, gain_ref, pool_ref, *rest):
    heads = q_ref.shape[0]
    prompts = q_ref.shape[1] // SEQ
    n_heads = pool_ref.shape[1]
    first = pair * heads
    out_ref, state_ref, state_scr = rest[-3:]
    ri = lax.broadcasted_iota(jnp.int32, (CHUNK, CHUNK), 0)
    ci = lax.broadcasted_iota(jnp.int32, (CHUNK, CHUNK), 1)
    diff = ri ^ ci
    lower = ri > ci
    eye = (ri == ci).astype(F32)
    causal = ri >= ci
    seqs = [(p, h) for p in range(prompts) for h in range(heads)]
    every = range(len(seqs))
    for n, (p, h) in enumerate(seqs):
        state_scr[n] = pool_ref[index[p * n_heads + first + h], first + h]

    @pl.loop(0, SEQ // CHUNK)
    def _(c):
        at = [pl.ds(pl.multiple_of(p * SEQ + c * CHUNK, CHUNK), CHUNK) for p in range(prompts)]
        q = [q_ref[h, at[p], :] for p, h in seqs]
        k = [k_ref[h, at[p], :] for p, h in seqs]
        v = [v_ref[h, at[p], :] for p, h in seqs]
        rate = [rate_ref[at[p], first + h : first + h + 1] for p, h in seqs]
        gram = [mm(k[n], k[n], ((1,), (1,))) for n in every]
        strict = [jnp.where(lower, gram[n] * rate[n], 0.0) for n in every]
        inv = [eye - jnp.where(diff == 1, strict[n], 0.0) for n in every]
        level = 1
        while (2 << level) <= CHUNK:
            part = [jnp.where((diff >> level) == 1, strict[n], 0.0).astype(BF) for n in every]
            low = [inv[n].astype(BF) for n in every]
            mid = [mm(part[n], low[n]).astype(BF) for n in every]
            inv = [inv[n] - mm(low[n], mid[n]) for n in every]
            level += 1
        scores = [
            jnp.where(causal, mm(q[n], k[n], ((1,), (1,))), 0.0).astype(BF) for n in every
        ]
        right = [
            jnp.concatenate(
                [(k[n].astype(F32) * rate[n]).astype(BF), (v[n].astype(F32) * rate[n]).astype(BF)],
                axis=1,
            )
            for n in every
        ]
        solved = [mm(inv[n].astype(BF), right[n]) for n in every]
        state = [state_scr[n] for n in every]
        both = [
            mm(
                jnp.concatenate([solved[n][:, :DK].astype(BF), q[n]], axis=0),
                state[n].astype(BF),
            )
            for n in every
        ]
        fixed = [(solved[n][:, DK:] - both[n][:CHUNK]).astype(BF) for n in every]
        for n in every:
            state_scr[n] = state[n] + mm(k[n], fixed[n], ((0,), (0,)))
        for n, (p, h) in enumerate(seqs):
            out = both[n][CHUNK:] + mm(scores[n], fixed[n])
            out = jnp.where(c * CHUNK + ri < lens[p], out, 0.0)
            scale = lax.rsqrt(jnp.mean(out * out, axis=1, keepdims=True) + 1e-05)
            gain = gain_ref[0:1, h * DK : (h + 1) * DK]
            out_ref[at[p], h * DK : (h + 1) * DK] = (out * scale * gain).astype(BF)

    for n, (p, h) in enumerate(seqs):
        state_ref[p, h] = state_scr[n]


def scan_pair(pair, lens, index, q, k, v, rate, gain, pool, state=None):
    heads = q.shape[0]
    prompts = lens.shape[0]
    n_heads = pool.shape[1]
    total = prompts * SEQ
    qkv = pl.BlockSpec((heads, total, DK), lambda p, n, i: (0, 0, 0))
    in_specs = [qkv] * 3 + [
        pl.BlockSpec((total, DK), lambda p, n, i: (0, 0)),
        pl.BlockSpec((1, heads * DK), lambda p, n, i: (0, pair)),
        pl.BlockSpec(pool.shape, lambda p, n, i: (0, 0, 0, 0)),
    ]
    operands = [lens, index, q, k, v, rate, gain, pool]
    aliases = {}
    if state is not None:
        aliases = {len(operands): 1}
        in_specs += [pl.BlockSpec(memory_space=pl.ANY)]
        operands += [state]
    grid_spec = pltpu.PrefetchScalarGridSpec(
        num_scalar_prefetch=2,
        grid=(1,),
        in_specs=in_specs,
        out_specs=[
            pl.BlockSpec((total, heads * DK), lambda p, n, i: (0, 0)),
            pl.BlockSpec((prompts, heads, DK, DK), lambda p, n, i: (0, pair, 0, 0)),
        ],
        scratch_shapes=[pltpu.VMEM((prompts * heads, DK, DK), F32)],
    )
    return pl.pallas_call(
        functools.partial(scan_kernel, pair),
        grid_spec=grid_spec,
        out_shape=[
            jax.ShapeDtypeStruct((prompts * SEQ, heads * DK), BF),
            jax.ShapeDtypeStruct((prompts, n_heads, DK, DK), F32),
        ],
        input_output_aliases=aliases,
        compiler_params=pltpu.CompilerParams(vmem_limit_bytes=56 << 20),
        cost_estimate=pl.CostEstimate(flops=12 << 30, bytes_accessed=6 << 20, transcendentals=0),
        name="delta",
    )(*operands)


def out_kernel(n_piece, spots, *refs):
    xs, refs = refs[: 2 * ROWS], refs[2 * ROWS :]
    halves = (refs[:n_piece], refs[n_piece : 2 * n_piece])
    o_ref, w_scr = refs[2 * n_piece :]
    width = w_scr.shape[2] // 2

    @pl.when(pl.program_id(0) == 0)
    def _():
        for s in range(2):
            assemble(spots.at[s], halves[s], w_scr, s * width)

    span = xs[0].shape[1]
    acc = 0.0
    for j in range(2):
        for r in range(ROWS):
            acc += mm(xs[j * ROWS + r][...], w_scr[r, j * span : (j + 1) * span, :])
    o_ref[...] = acc.astype(BF)


def out_product(spots, xs, halves, in_cols, out_cols):
    total, span = xs[0].shape

    def tail(x):
        return pl.BlockSpec(
            (x.shape[0], x.shape[1], out_cols), lambda p, c: (0, 0, in_cols // out_cols)
        )

    grid_spec = pltpu.PrefetchScalarGridSpec(
        num_scalar_prefetch=1,
        grid=(total // SEQ,),
        in_specs=[pl.BlockSpec((SEQ, span), lambda p, c: (p, 0))] * (2 * ROWS)
        + [tail(x) for half in halves for x in half],
        out_specs=pl.BlockSpec((SEQ, 2 * out_cols), lambda p, c: (p, 0)),
        scratch_shapes=[pltpu.VMEM((ROWS, spots.shape[1] * 16, 2 * out_cols), BF)],
    )
    return pl.pallas_call(
        functools.partial(out_kernel, len(halves[0])),
        grid_spec=grid_spec,
        out_shape=jax.ShapeDtypeStruct((total, 2 * out_cols), BF),
        compiler_params=pltpu.CompilerParams(vmem_limit_bytes=32 << 20),
        cost_estimate=pl.CostEstimate(
            flops=4 * total * 2048 * out_cols, bytes_accessed=10 << 20, transcendentals=0
        ),
        name="outmix",
    )(spots, *xs, *halves[0], *halves[1])


def place_kernel(source, x0, x1, after, o_ref):
    width = x0.shape[2]
    for j, ref in enumerate((x0, x1)):
        o_ref[0, :, :, j * width : (j + 1) * width] = ref[0].reshape(PAGE, 2, width)


def place_pages(source, came0, came1, n_pages, after):
    width = came0.shape[2]
    spec = pl.BlockSpec((1, 2 * PAGE, width), lambda i, s: (s[i], 0, 0))
    grid_spec = pltpu.PrefetchScalarGridSpec(
        num_scalar_prefetch=1,
        grid=(n_pages,),
        in_specs=[spec, spec, pl.BlockSpec(memory_space=pl.ANY)],
        out_specs=pl.BlockSpec((1, PAGE, 2, 2 * width), lambda i, s: (i, 0, 0, 0)),
    )
    return pl.pallas_call(
        place_kernel,
        grid_spec=grid_spec,
        out_shape=jax.ShapeDtypeStruct((n_pages, PAGE, 2, 2 * width), BF),
        cost_estimate=pl.CostEstimate(flops=0, bytes_accessed=6 << 20, transcendentals=0),
        name="place",
    )(source, came0, came1, after)


def hold_kernel(*refs):
    pass


def hold_back(x, *after):
    spec = pl.BlockSpec(memory_space=pl.ANY)
    return pl.pallas_call(
        hold_kernel,
        in_specs=[spec] * (1 + len(after)),
        out_specs=spec,
        out_shape=jax.ShapeDtypeStruct(x.shape, x.dtype),
        input_output_aliases={0: 0},
        name="hold",
    )(x, *after)


def col_place(c):
    return c // 8, (c // 4) % 2, c % 4


def col_index(y, x, z):
    return (y % 4) * 8 + (x % 2) * 4 + z % 4


def col_shift(x, dy, dz):
    def to(c):
        py, px, pz = col_place(c)
        return col_index(py + dy, px, pz + dz)

    return lax.ppermute(x, "col", [(c, to(c)) for c in range(32)])


def ring_pieces(x, axis):
    step = (1, 0) if axis == "y" else (0, 1)
    back = (-step[0], -step[1])
    before = col_shift(x, *step)
    after = col_shift(x, *back)
    half = x.shape[0] // 2
    return [x, before, col_shift(before[:half], *step), col_shift(after[half:], *back), after]


def spots_for(col, first):
    offsets = (0, -1, -2, 1)
    py, px, pz = col_place(col)
    table = []
    for outer in offsets:
        for inner in offsets:
            for flip in range(2):
                dy, dz = (outer, inner) if first == "z" else (inner, outer)
                table.append(((py + dy) % 4) * 8 + (px ^ flip) * 4 + (pz + dz) % 4)
    return jnp.stack(table).astype(jnp.int32)


def gather_half(x, first):
    second = "y" if first == "z" else "z"
    return ring_pieces(jnp.concatenate(ring_pieces(x, first), axis=0), second)


def row_swap(x, k):
    return lax.ppermute(x, "row", [(r, r ^ k) for r in range(ROWS)])


def row_gather(x):
    near = row_swap(x, 2)
    return [x, near, row_swap(x, 1), row_swap(near, 1)]


def local(
    tokens,
    in_weight,
    out_weight,
    beta_weight,
    conv_weight,
    conv_prior,
    head_gain,
    state_pool,
    state_index,
    lengths,
    page_table,
):
    n_col = lax.axis_size("col")
    row_id = lax.axis_index("row")
    span = tokens.shape[1]
    heads = state_index.shape[1]
    prompts = lengths.shape[0]
    n_pages = prompts * PAGES_SEQ
    part = in_weight.shape[0]
    in_cols = in_weight.shape[1] // ROWS
    out_cols = out_weight.shape[1] // ROWS

    win = in_weight.astype(BF)
    wout = out_weight.astype(BF)
    half_in, half_out = in_cols // 2, out_cols // 2
    both = jnp.concatenate(
        [win.reshape(part, ROWS, 2, half_in), wout.reshape(part, ROWS, 2, half_out)], axis=3
    ).transpose(1, 0, 2, 3)
    both = both.reshape(ROWS, part, in_cols + out_cols)
    by_xor = [lax.dynamic_index_in_dim(both, row_id ^ k, 0, keepdims=False) for k in XORS]

    def swap(x, k, flip):
        pairs = [
            (r * 32 + c, (r ^ k) * 32 + (c ^ (4 * flip))) for r in range(ROWS) for c in range(32)
        ]
        return lax.ppermute(x, ("row", "col"), pairs)

    rows = [
        by_xor[i] if k == 0 and flip == 0 else swap(by_xor[i], k, flip)
        for flip in range(2)
        for i, k in enumerate(XORS)
    ]
    mine = jnp.concatenate(rows, axis=0).reshape(2, ROWS * part, in_cols + out_cols)
    cut = half_in + half_out
    halves = [gather_half(mine[:, :, :cut], "z"), gather_half(mine[:, :, cut:], "y")]
    col_id = lax.axis_index("col")
    spots = [spots_for(col_id, "z"), spots_for(col_id, "y")]
    toks = row_gather(tokens)

    targets = page_table[:, :, 0].reshape(-1)
    slots = page_table[:, :, 1].reshape(-1)
    beta = lax.dynamic_slice_in_dim(beta_weight, row_id * heads, heads, 1).astype(BF)
    beta = beta.reshape(ROWS, span, heads)
    beta = jnp.stack(
        [lax.dynamic_index_in_dim(beta, row_id ^ k, 0, keepdims=False) for k in XORS]
    )
    beta = jnp.pad(beta, ((0, 0), (0, 0), (0, DK - heads)))
    prior = jnp.pad(conv_prior.astype(F32), ((0, 0), (8 - (CONV - 1), 0), (0, 0)))

    q0, k0, v0, out0, rate = project(
        0, targets, lengths, spots[0], toks, halves[0], beta, conv_weight, prior, n_col,
        halves[1][1:],
    )
    came0 = lax.all_to_all(out0, "col", split_axis=0, concat_axis=0, tiled=True)
    states = state_index.reshape(-1)
    gain = head_gain.reshape(1, -1)
    normed0, state0 = scan_pair(0, lengths, states, q0, k0, v0, rate, gain, state_pool)
    q1, k1, v1, out1 = project(
        1, targets, lengths, spots[1], toks, halves[1], None, conv_weight, prior, n_col, [normed0]
    )
    heads0 = row_gather(normed0)
    normed1, final_state = scan_pair(
        1, lengths, states, q1, k1, v1, rate, gain, state_pool, state0
    )
    heads1 = row_gather(normed1)
    hit = targets[:, None] == jnp.arange(n_col, dtype=jnp.int32)[None, :]
    slot_for = jnp.max(jnp.where(hit, slots[:, None], -1), axis=0)
    block_in, block_out = win.shape[1] // n_col, wout.shape[1] // n_col
    send = jnp.concatenate(
        [
            win.reshape(part, n_col, block_in).transpose(1, 0, 2).reshape(n_col, -1, DK),
            wout.reshape(part, n_col, block_out).transpose(1, 0, 2).reshape(n_col, -1, DK),
            jnp.broadcast_to(slot_for.astype(BF)[:, None, None], (n_col, 8, DK)),
        ],
        axis=1,
    )
    send = hold_back(send, came0)
    got = lax.all_to_all(send, "col", split_axis=0, concat_axis=0, tiled=True)
    n_in = part * block_in // DK
    n_out = part * block_out // DK
    server_in = got[:, :n_in].reshape(n_col * part, block_in)
    server_out = got[:, n_in : n_in + n_out].reshape(n_col * part, block_out)
    arrived_slots = got[:, n_in + n_out, 0].astype(jnp.int32)
    wanted = arrived_slots[None, :] == jnp.arange(n_pages, dtype=jnp.int32)[:, None]
    source = jnp.sum(
        jnp.where(wanted, jnp.arange(n_col, dtype=jnp.int32)[None, :], 0), axis=1
    ).astype(jnp.int32)

    out1 = hold_back(out1, got, heads0[1], heads1[1])
    came1 = lax.all_to_all(out1, "col", split_axis=0, concat_axis=0, tiled=True)
    layer_out = out_product(
        jnp.stack(spots), heads0 + heads1, halves, half_in, half_out
    )
    page_cache = place_pages(source, came0, came1, n_pages, layer_out)
    return (server_in, server_out, layer_out, final_state, page_cache)


def solution(mesh):
    return jax.shard_map(
        local,
        mesh=mesh,
        in_specs=(
            P("col", "row"),
            P(("row", "col"), None),
            P(("row", "col"), None),
            P(),
            P(None, "row"),
            P("col", None, "row"),
            P("row"),
            P("col", "row", None, None),
            P("col", "row"),
            P("col"),
            P("col", None, None),
        ),
        out_specs=(
            P("row", "col"),
            P("row", "col"),
            P("col", "row"),
            P("col", "row", None, None),
            P("col", None, None, "row"),
        ),
        check_vma=False,
    )
```
